256 devices in a mesh: row: 8 (over x, core), col: 32 (over y, z).
Axes of the slice: x: 4, y: 4, z: 8, core: 2. Of those that a mesh axis runs over, the one named last changes fastest.
Arguments:
- hidden: bfloat16 [128, 8192], P('col', 'row'), may hold values from -6 to 6
- w_gate: bfloat16 [8192, 16384], P('row', 'col'), may hold values from -0.0625 to 0.0625
- w_up: bfloat16 [8192, 16384], P('row', 'col'), may hold values from -0.0625 to 0.0625
- prior: float32 [16384, 16384], P('row', 'col'), may hold values from -1 to 12, as said below
- rhs: float32 [16384, 4096], P('row', 'col'), may hold values from -6 to 6
Outputs:
- factored: float32 [16384, 16384], P('row', 'col')
- right_out: float32 [16384, 4096], P('row', 'col')
The draws below stay inside these ranges and needn't reach their ends.
Inputs may be any that keep to these rules, and one draw needn't show every extreme that they name: prior is symmetric and positive definite, with smallest eigenvalue 0.1 or more.
All inputs are finite; a program needn't handle non-finite values.
Results may differ from the reference program's by a relative error of at most 0.0003.
Values may be sent and summed in bfloat16 or wider, within the bound.
No kernel may reach another device: no remote copies, remote signals or barrier semaphores. Data moves between devices by JAX's collectives and lax.ppermute only.
A program may use at most 64 MiB of HBM per device.

```python
import math
import jax
import jax.numpy as jnp
from jax import lax

D = 8192
KW = 16384
E = 4096
P_SIZE = 128
PANELS = 2
R = 128


def draw_prior(key, part):
    first = jax.random.fold_in(key, 11)
    second = jax.random.fold_in(key, 12)
    noise = jax.random.normal(first, (KW, KW), jnp.float32)
    base = (noise + noise.T) * (0.3 / math.sqrt(2.0 * KW))
    diagonal = jax.random.uniform(second, (KW,), jnp.float32, 1.0, 3.0)
    index = jnp.arange(KW, dtype=jnp.int32)
    base = base.at[index, index].add(diagonal)
    return base


def level_of(rng, shape, shards, smallest, largest):
    loudness = 1.0
    for axis_at, shards_of in shards:
        steps = jax.random.uniform(jax.random.fold_in(jax.random.fold_in(rng, 6), axis_at), (shards_of,), jnp.float32, smallest / len(shards), largest / len(shards))
        loudness = loudness * jnp.repeat(jnp.exp(steps), shape[axis_at] // shards_of).reshape((-1,) + (1,) * (len(shape) - 1 - axis_at))
    return loudness


def gaussian(rng, shape, width, reach, split=(), kind=jnp.bfloat16):
    array = jax.random.normal(rng, shape, jnp.float32) * width
    if len(split) > 0:
        array = level_of(rng, shape, split, -0.22, 0.18) * array
    return jnp.clip(array, min=-reach, max=reach).astype(kind)


def setup_inputs(seed: int = 0) -> dict:
    splits = jax.random.split(jax.random.key(seed), 6)
    return {
        "hidden": gaussian(splits[0], (R, D), 1.0, 6.0, ((0, 32), (1, 8))),
        "w_gate": gaussian(splits[1], (D, KW), D ** -0.5, 0.0625, ((0, 8), (1, 32))),
        "w_up": gaussian(splits[2], (D, KW), D ** -0.5, 0.0625, ((0, 8), (1, 32))),
        "prior": draw_prior(jax.random.fold_in(splits[5], 71), 0),
        "rhs": gaussian(splits[4], (KW, E), 1.0, 6.0, ((0, 8), (1, 32)), jnp.float32),
    }


DAMP = 0.5

def reference(hidden, w_gate, w_up, prior, rhs):
    gate = jnp.dot(hidden.astype(jnp.float32), w_gate.astype(jnp.float32), preferred_element_type=jnp.float32)
    upward = jnp.dot(hidden.astype(jnp.float32), w_up.astype(jnp.float32), preferred_element_type=jnp.float32)
    keys = jax.nn.silu(gate) * upward
    outer = jnp.dot(keys.T.astype(jnp.float32), keys.astype(jnp.float32), precision=lax.Precision.HIGHEST, preferred_element_type=jnp.float32)
    work = prior + outer / R
    index = jnp.arange(KW, dtype=jnp.int32)
    work = work.at[index, index].add(DAMP)
    right = rhs
    offsets = jnp.arange(P_SIZE, dtype=jnp.int32)
    below_diag = offsets[:, None] >= offsets[None, :]
    for panel in range(PANELS):
        start = panel * P_SIZE
        stop = start + P_SIZE
        pivot = jnp.linalg.cholesky(work[start:stop, start:stop])
        below = jax.scipy.linalg.solve_triangular(pivot, work[stop:, start:stop].T, lower=True).T
        solution = jax.scipy.linalg.solve_triangular(pivot, right[start:stop], lower=True)
        work = work.at[stop:, stop:].add(-jnp.dot(below.astype(jnp.float32), below.T.astype(jnp.float32), precision=lax.Precision.HIGHEST, preferred_element_type=jnp.float32))
        right = right.at[stop:].add(-jnp.dot(below.astype(jnp.float32), solution.astype(jnp.float32), precision=lax.Precision.HIGHEST, preferred_element_type=jnp.float32))
        right = right.at[start:stop].set(solution)
        block = jnp.where(below_diag, pivot, work[start:stop, start:stop])
        work = work.at[start:stop, start:stop].set(block)
        work = work.at[stop:, start:stop].set(below)
    return (work, right)
```

```python
import functools

import jax
import jax.numpy as jnp
from jax import lax
from jax.experimental import pallas as pl
from jax.experimental.pallas import tpu as pltpu
from jax.sharding import Mesh
from jax.sharding import PartitionSpec as P

P_SIZE = 128
WIDE = 256
DAMP = 0.5
ROWS, YS, ZS = 8, 4, 8
COL = ("col_0", "col_1")
ALL = ("row", "col_0", "col_1")
HIGHEST = lax.Precision.HIGHEST
NN = (((1,), (0,)), ((), ()))
TN = (((0,), (0,)), ((), ()))
NT = (((1,), (1,)), ((), ()))


def copies(shard, axis):
    peers = lax.axis_size(axis)
    wide = jnp.broadcast_to(shard[None], (peers, *shard.shape))
    return lax.all_to_all(wide, axis, 0, 0, tiled=True)


def row_tree(x):
    at = lax.axis_index("row")
    for step in (4, 2, 1):
        pairs = [(i, i + step) for i in range(0, ROWS, 2 * step)]
        got = lax.ppermute(x, "row", pairs)
        x = jnp.where(at % (2 * step) == step, got, x)
    return x


def col_tree(x):
    at = lax.axis_index(COL)
    for step in (4, 2, 1):
        pairs = [(i, i + step) for i in range(0, ZS, 2 * step)]
        got = lax.ppermute(x, COL, pairs)
        x = jnp.where(at % (2 * step) == step, got, x)
    for step in (2 * ZS, ZS):
        pairs = [(i + z, i + step + z) for i in range(0, YS * ZS, 2 * step) for z in range(ZS)]
        got = lax.ppermute(x, COL, pairs)
        x = jnp.where(at // ZS * ZS % (2 * step) == step, got, x)
    return x


def to_row_blocks(piece):
    cols = YS * ZS
    pairs = [
        (k * cols + c, (c // YS) * cols + ZS * (c % YS) + k) for k in range(ROWS) for c in range(cols)
    ]
    return lax.ppermute(piece, ALL, pairs)


def gather_row_blocks(piece):
    return copies(copies(to_row_blocks(piece), "col_1"), "col_0")


def split(x):
    high = x.astype(jnp.bfloat16)
    return high, (x - high.astype(jnp.float32)).astype(jnp.bfloat16)


def dot3(a, b, dims):
    ah, al = a
    bh, bl = b
    dot = functools.partial(lax.dot_general, dimension_numbers=dims, preferred_element_type=jnp.float32)
    return dot(ah, bh) + (dot(ah, bl) + dot(al, bh))


def finish_kernel(
    at_ref, prior_ref, rhs_ref, keys_ref, panel_ref, mine_ref, across_ref, first_ref, inverse_ref,
    pivot_ref, solved_ref, out_ref, right_ref,
):
    step = pl.program_id(0)
    row_id = at_ref[0]
    col_id = at_ref[1]
    samples, tall = keys_ref.shape[1:]
    wide = prior_ref.shape[1]
    row_at = (row_id * pl.num_programs(0) + step) * tall
    col_at = col_id * wide
    keys = keys_ref[0]
    scaled = keys * (1.0 / samples)
    first = split(first_ref[...])
    inverse = split(inverse_ref[...])
    scaled_parts = split(scaled)
    crossing = panel_ref[0] + dot3(first, scaled_parts, TN)
    solved = dot3(inverse, split(crossing), NN)
    line = lax.broadcasted_iota(jnp.int32, solved.shape, 0) // P_SIZE
    below = row_at + lax.broadcasted_iota(jnp.int32, solved.shape, 1) >= (line + 1) * P_SIZE
    solved = jnp.where(below, solved, 0.0)
    solved_parts = split(-solved)
    block = prior_ref[...] + dot3(scaled_parts, split(mine_ref[...]), TN)
    block = block + dot3(solved_parts, split(across_ref[...]), TN)
    row = row_at + lax.broadcasted_iota(jnp.int32, block.shape, 0)
    col = col_at + lax.broadcasted_iota(jnp.int32, block.shape, 1)
    out_ref[...] = jnp.where(row == col, block + DAMP, block)
    right_ref[...] = rhs_ref[...] + dot3(solved_parts, split(solved_ref[...]), TN)

    @pl.when(col_id == 0)
    def _():
        own = prior_ref[:, :WIDE] + dot3(scaled_parts, first, TN)
        own = dot3(split(own), inverse, NT)
        row = row_at + lax.broadcasted_iota(jnp.int32, own.shape, 0)
        out_ref[:, :WIDE] = jnp.where(row >= WIDE, own, out_ref[:, :WIDE])

    @pl.when(row_at == 0)
    def _():
        right_ref[:WIDE, :] = solved_ref[...]

        @pl.when(col_id == 0)
        def _():
            row = lax.broadcasted_iota(jnp.int32, (WIDE, WIDE), 0)
            col = lax.broadcasted_iota(jnp.int32, (WIDE, WIDE), 1)
            out_ref[:WIDE, :WIDE] = jnp.where(row >= col, pivot_ref[...], out_ref[:WIDE, :WIDE])


def finish(at, prior, rhs, keys, panel, mine, across, first, inverse, pivot, solved):
    height, width = prior.shape
    blocks, samples, tall = keys.shape
    whole = lambda a: pl.BlockSpec(a.shape, lambda i: (0,) * a.ndim)
    return pl.pallas_call(
        finish_kernel,
        grid=(blocks,),
        in_specs=[
            pl.BlockSpec(memory_space=pltpu.SMEM),
            pl.BlockSpec((tall, width), lambda i: (i, 0)),
            pl.BlockSpec((tall, rhs.shape[1]), lambda i: (i, 0)),
            pl.BlockSpec((1, samples, tall), lambda i: (i, 0, 0)),
            pl.BlockSpec((1, WIDE, tall), lambda i: (i, 0, 0)),
            whole(mine),
            whole(across),
            whole(first),
            whole(inverse),
            whole(pivot),
            whole(solved),
        ],
        out_specs=[
            pl.BlockSpec((tall, width), lambda i: (i, 0)),
            pl.BlockSpec((tall, rhs.shape[1]), lambda i: (i, 0)),
        ],
        out_shape=[
            jax.ShapeDtypeStruct(prior.shape, jnp.float32),
            jax.ShapeDtypeStruct(rhs.shape, jnp.float32),
        ],
        compiler_params=pltpu.CompilerParams(
            dimension_semantics=("arbitrary",), vmem_limit_bytes=48 * 1024 * 1024
        ),
        name="finish",
    )(at, prior, rhs, keys, panel, mine, across, first, inverse, pivot, solved)


def mul(a, b, dims=NN):
    return lax.dot_general(a, b, dims, precision=HIGHEST, preferred_element_type=jnp.float32)


def factor(block):
    half = P_SIZE
    eye = jnp.eye(half, dtype=jnp.float32)
    first = lax.linalg.cholesky(block[:half, :half], symmetrize_input=False)
    first_inv = jax.scipy.linalg.solve_triangular(first, eye, lower=True)
    side = mul(block[half:, :half], first_inv, NT)
    second = lax.linalg.cholesky(block[half:, half:] - mul(side, side, NT), symmetrize_input=False)
    second_inv = jax.scipy.linalg.solve_triangular(second, eye, lower=True)
    side_inv = -mul(mul(second_inv, side), first_inv)
    none = jnp.zeros((half, half), jnp.float32)
    pivot = jnp.block([[first, none], [side, second]])
    inverse = jnp.block([[first_inv, none], [side_inv, second_inv]])
    return pivot, inverse


def local(hidden, w_gate, w_up, prior, rhs):
    row_id = lax.axis_index("row")
    col_id = lax.axis_index(COL)
    height, width = prior.shape

    tokens = copies(hidden, COL).reshape(-1, hidden.shape[1])
    samples = tokens.shape[0]

    top = row_tree(jnp.concatenate([prior[:WIDE], rhs[:WIDE]], axis=1))
    panel_cols, head = top[:, :width], top[:, width:]
    diagonal = col_tree(panel_cols[:, :WIDE])
    slab = WIDE // ROWS
    piece = lax.dynamic_slice_in_dim(panel_cols, row_id * slab, slab, 0).astype(jnp.float16)
    panel = gather_row_blocks(piece).reshape(YS, WIDE, width).astype(jnp.float32)

    gate_part = jnp.dot(tokens, w_gate, preferred_element_type=jnp.float32)
    up_part = jnp.dot(tokens, w_up, preferred_element_type=jnp.float32)
    parts = jnp.concatenate([gate_part, up_part], axis=1).reshape(ROWS, samples // ROWS, 2 * width)
    sums = lax.all_to_all(parts, "row", 0, 0, tiled=True).sum(0)
    mine = jax.nn.silu(sums[:, :width]) * sums[:, width:]

    keys_rows = gather_row_blocks(mine).reshape(YS, samples, width)
    keys_cols = copies(mine, "row").reshape(samples, width)
    first = col_tree(keys_cols[:, :WIDE])

    eye = jnp.eye(WIDE, dtype=jnp.float32)
    pivot, inverse = factor(diagonal + mul(first, first, TN) / samples + DAMP * eye)
    cross = panel_cols + mul(first, keys_cols, TN) / samples
    across = mul(inverse, cross)
    col_global = col_id * width + lax.iota(jnp.int32, width)
    line = lax.iota(jnp.int32, WIDE) // P_SIZE
    across = jnp.where(col_global[None, :] >= (line[:, None] + 1) * P_SIZE, across, 0.0)
    solved = mul(inverse, head)
    at = jnp.stack([row_id, col_id]).astype(jnp.int32)
    return finish(
        at, prior, rhs, keys_rows, panel, keys_cols, across, first, inverse, pivot, solved
    )


def solution(mesh):
    finer = Mesh(mesh.devices.reshape(ROWS, YS, ZS), ALL)
    return jax.shard_map(
        local,
        mesh=finer,
        in_specs=(P(COL, "row"), P("row", COL), P("row", COL), P("row", COL), P("row", COL)),
        out_specs=(P("row", COL), P("row", COL)),
        check_vma=False,
    )
```
